512 devices in a mesh: row: 16 (over z_hi, y, core), col: 32 (over z_lo, x).
Axes of the slice: x: 4, y: 4, z: 16 (z_hi: 2, z_lo: 8; z = z_hi * 8 + z_lo), core: 2. Of those that a mesh axis runs over, the one named last changes fastest.
Arguments:
- query_grads: bfloat16 [256, 8192], P('row', 'col'), may hold values from -6 to 6
- query_acts: bfloat16 [256, 8192], P('col', 'row'), may hold values from -6 to 6
- train_grads: bfloat16 [512, 8192], P('row', 'col'), may hold values from -6 to 6
- train_acts: bfloat16 [512, 8192], P('col', 'row'), may hold values from -6 to 6
- grad_basis: bfloat16 [8192, 8192], P('col', 'row'), may hold values from -0.0625 to 0.0625
- act_basis: bfloat16 [8192, 8192], P('row', 'col'), may hold values from -0.0625 to 0.0625
- eigen_corr: float32 [8192, 8192], P('row', 'col'), may hold values from 0.02 to 2
- damping: float32 [], replicated, may hold values from 0.05 to 0.5
- query_seq: int32 [256], replicated, may hold values from 0 to 31, never falling along the last dimension, each value on 1 to 16 neighbouring positions
- train_doc: int32 [512], replicated, may hold values from 0 to 15, never falling along the last dimension, each value on 1 to 64 neighbouring positions
Outputs:
- scores: float32 [32, 512], P(None, 'col')
- doc_scores: float32 [32, 16], replicated
The draws below stay inside these ranges and needn't reach their ends.
Inputs may be any that keep to these rules, and one draw needn't show every extreme that they name: `query_seq`: Non-decreasing along the query tokens; every sequence has 1 to 16 tokens, and one has exactly that many. `train_doc`: Non-decreasing along the training tokens; every document has 1 to 64 tokens, and one has exactly that many.
All inputs are finite; a program needn't handle non-finite values.
Results may differ from the reference program's by a relative error of at most 0.005.
Values may be sent and summed in bfloat16 or wider, within the bound.
No kernel may reach another device: no remote copies, remote signals or barrier semaphores. Data moves between devices by JAX's collectives and lax.ppermute only.
A program may use at most 64 MiB of HBM per device.

```python
import math
import jax
import jax.numpy as jnp
import numpy as np
from jax import lax

D = 8192
S = 32
QTOK = 256
UTOK = 512
DOCS = 16


def block_scale(rng, dims, split, least, largest):
    factor_of, own = 1.0, jax.random.fold_in(rng, 6)
    for position, shards_of in split:
        steps = jnp.exp(jax.random.uniform(jax.random.fold_in(own, position), (shards_of,), jnp.float32, least / len(split), largest / len(split)))
        factor_of = factor_of * jnp.repeat(steps, dims[position] // shards_of).reshape([-1 if axis == position else 1 for axis in range(len(dims))])
    return factor_of


def length_profile(count, total, most, lean):
    loads = [(1 << 20) // math.isqrt(standing ** lean) + 1 for standing in range(2, count + 1)]
    spare, holding = total - most - (count - 1), [1] * (count - 1)
    while spare > 0:
        candidates = [i for i in range(count - 1) if holding[i] < most]
        mass, remaining = sum([loads[i] for i in candidates]), spare
        for i in candidates:
            addition = min(most - holding[i], max(1, remaining * loads[i] // mass), spare)
            holding[i] = holding[i] + addition
            spare = spare - addition
    return np.array([most] + holding)


def uneven(stream_key, count, total, limit, skew):
    if count == 2:
        one = jax.random.randint(stream_key, (), max(1, total - limit), min(limit, total - 1) + 1)
        return jnp.stack([one, total - one])
    lengths = jnp.asarray(length_profile(count, total, limit, skew), jnp.int32)
    pairs = (count - 1) // 2
    donor, taker = lengths[1:1 + 2 * pairs:2], lengths[2:2 + 2 * pairs:2]
    margin = jnp.minimum(donor - 1, limit - taker)
    shifted = jax.random.randint(jax.random.fold_in(stream_key, 1), (pairs,), 0, 1 << 20) % (margin + 1)
    lengths = lengths.at[1:1 + 2 * pairs:2].set(donor - shifted).at[2:2 + 2 * pairs:2].set(taker + shifted)
    return lengths[jax.random.permutation(jax.random.fold_in(stream_key, 2), count)]


def normal_values(key, shape, width, bound, split=(), held_as=jnp.bfloat16):
    array = jax.random.normal(key, shape, jnp.float32) * width
    if len(split) > 0:
        array = block_scale(key, shape, split, -0.22, 0.18) * array
    return jnp.clip(array, min=-bound, max=bound).astype(held_as)


def setup_inputs(seed: int = 0) -> dict:
    arg_keys = jax.random.split(jax.random.key(seed), 11)
    query_grads = normal_values(arg_keys[0], (QTOK, D), 1.0, 6.0, ((0, 16), (1, 32)))
    query_acts = normal_values(arg_keys[1], (QTOK, D), 1.0, 6.0, ((0, 32), (1, 16)))
    train_grads = normal_values(arg_keys[2], (UTOK, D), 1.0, 6.0, ((0, 16), (1, 32)))
    train_acts = normal_values(arg_keys[3], (UTOK, D), 1.0, 6.0, ((0, 32), (1, 16)))
    grad_basis = normal_values(arg_keys[4], (D, D), D ** -0.5, 0.0625, ((0, 32), (1, 16)))
    act_basis = normal_values(arg_keys[5], (D, D), D ** -0.5, 0.0625, ((0, 16), (1, 32)))
    eigen_corr = jnp.clip(jnp.exp(math.log(2.0) - 4.6051702 * jax.random.uniform(arg_keys[6], (D, D), jnp.float32) ** block_scale(arg_keys[6], (D, D), ((0, 16), (1, 32)), -0.2, 0.2)), 0.02, 2.0)
    damping = jnp.clip(jax.random.uniform(arg_keys[7], (), jnp.float32, 0.05, 0.5), 0.05, 0.5)
    query_seq = jnp.searchsorted(jnp.cumsum(uneven(arg_keys[8], S, QTOK, 2 * QTOK // S, 1)), jnp.arange(QTOK), side="right").astype(jnp.int32)
    train_doc = jnp.searchsorted(jnp.cumsum(uneven(arg_keys[9], DOCS, UTOK, 2 * UTOK // DOCS, 1)), jnp.arange(UTOK), side="right").astype(jnp.int32)
    return {"query_grads": query_grads, "query_acts": query_acts, "train_grads": train_grads, "train_acts": train_acts, "grad_basis": grad_basis, "act_basis": act_basis, "eigen_corr": eigen_corr, "damping": damping, "query_seq": query_seq, "train_doc": train_doc}


def reference(query_grads, query_acts, train_grads, train_acts, grad_basis, act_basis, eigen_corr, damping, query_seq, train_doc):
    grad_query = jnp.dot(query_grads, grad_basis, preferred_element_type=jnp.float32).astype(jnp.bfloat16)
    grad_train = jnp.dot(train_grads, grad_basis, preferred_element_type=jnp.float32).astype(jnp.bfloat16)
    act_query = jnp.dot(query_acts, act_basis, preferred_element_type=jnp.float32).astype(jnp.bfloat16)
    act_train = jnp.dot(train_acts, act_basis, preferred_element_type=jnp.float32).astype(jnp.bfloat16)
    denom = eigen_corr + damping
    act_wide = act_train.astype(jnp.float32)

    def one_sequence(seq_index):
        member = (query_seq == seq_index).astype(jnp.bfloat16)
        weighted = grad_query * member[:, None]
        outer = jnp.dot(weighted.T, act_query, preferred_element_type=jnp.float32)
        precond = (outer / denom).astype(jnp.bfloat16)
        mapped = jnp.dot(grad_train, precond, preferred_element_type=jnp.float32)
        return jnp.sum(mapped * act_wide, axis=1) / D

    scores = lax.map(one_sequence, jnp.arange(S, dtype=jnp.int32))
    doc_table = (train_doc[:, None] == jnp.arange(DOCS, dtype=jnp.int32)[None, :]).astype(jnp.float32)
    counts = jnp.sum(doc_table, axis=0)
    doc_sum = jnp.dot(scores, doc_table, precision=lax.Precision.HIGHEST)
    return scores, doc_sum / counts[None, :]
```

```python
import jax
import jax.numpy as jnp
from jax import lax
from jax.sharding import Mesh, PartitionSpec as P


D = 8192
S = 32
DOCS = 16
ROW = ("zh", "y", "c")
COL = ("zl", "x")


def spread(v, axes):
    n = lax.axis_size(axes)
    return lax.all_to_all(jnp.broadcast_to(v[None], (n,) + v.shape), axes, 0, 0, tiled=True)


def exchange(parts, axes):
    return lax.all_to_all(parts, axes, 0, 0, tiled=True)


def split(v):
    hi = lax.reduce_precision(v, 8, 7)
    return hi.astype(jnp.bfloat16), (v - hi).astype(jnp.bfloat16)


def shift(v, axis, k):
    n = lax.axis_size(axis)
    return lax.ppermute(v, axis, [(i, (i + k) % n) for i in range(n)])


def around(v, axis):
    n = lax.axis_size(axis)
    return jnp.stack([v] + [shift(v, axis, n - k) for k in range(1, n)])


def turn(v, axis):
    n = lax.axis_size(axis)
    return lax.dynamic_slice_in_dim(
        jnp.concatenate([v, v[: n - 1]], axis=0), (n - lax.axis_index(axis)) % n, n, 0
    )


def body(
    query_grads,
    query_acts,
    train_grads,
    train_acts,
    grad_basis,
    act_basis,
    eigen_corr,
    damping,
    query_seq,
    train_doc,
):
    bf16, f32 = jnp.bfloat16, jnp.float32
    n_query, n_train = query_seq.shape[0], train_doc.shape[0]
    nx, nzl, nzh = lax.axis_size("x"), lax.axis_size("zl"), lax.axis_size("zh")
    nyc = lax.axis_size(("y", "c"))
    q, t = query_acts.shape[0], train_acts.shape[0]
    n = q + t
    fi, fj = eigen_corr.shape

    a = spread(jnp.concatenate([query_acts, train_acts], axis=0), "zl")
    a = spread(a, "x")
    act_part = jnp.dot(a.reshape(-1, a.shape[-1]), act_basis, preferred_element_type=f32)
    act_part = act_part.astype(bf16).reshape(nyc, -1, fj)
    a = exchange(act_part, ("y", "c"))
    a = jnp.sum(a.astype(f32), axis=0)
    a = (a + lax.ppermute(a, "zh", [(0, 1), (1, 0)])).astype(bf16)
    a = around(a, "y")
    a = lax.all_gather(a, "c")
    acts = turn(jnp.swapaxes(a, 0, 1), "y").reshape(nx, nzl, n, fj)

    g = jnp.concatenate(
        [query_grads[:q], train_grads[:t], query_grads[q:], train_grads[t:]], axis=0
    )
    other = lax.ppermute(g, "zh", [(0, 1), (1, 0)])
    first = lax.axis_index("zh") == 0
    g = jnp.concatenate([jnp.where(first, g, other), jnp.where(first, other, g)], axis=0)
    g = around(g, "y")
    g = lax.all_gather(g, "c")
    g = g.reshape(n_query + n_train, -1)
    grad_part = jnp.dot(g, grad_basis, preferred_element_type=f32)
    grad_part = grad_part.astype(bf16).reshape(nx, -1, fi)
    x = lax.axis_index("x")
    own = [lax.dynamic_index_in_dim(grad_part, (x + k) % nx, 0, False) for k in range(nx)]
    got = [own[0]] + [shift(own[k], "x", k) for k in (1, nx - 1, 2)]
    g = sum(v.astype(f32) for v in got)
    g_hi, g_lo = split(g.reshape(nzl, n, fi))
    g = exchange(jnp.concatenate([g_hi, g_lo[:, :q]], axis=1), "zl").astype(f32)
    g = jnp.sum(g, axis=0)
    g = jnp.concatenate([g[:q] + g[n:], g[q:n]], axis=0).astype(bf16)
    g = spread(g, "zl").reshape(-1, fi)
    g = spread(g, "x")
    g = g.reshape(2, -1, nzh, 2, n, fi)
    grads = turn(jnp.moveaxis(g, 0, 2), "y")
    grads = jnp.swapaxes(grads, 0, 1)

    acts = jnp.swapaxes(acts, 0, 1)
    rot_gq = grads[..., :q, :].reshape(n_query, fi)
    rot_gu = grads[..., q:, :].reshape(n_train, fi)
    rot_aq = acts[:, :, :q].reshape(n_query, fj)
    rot_au = acts[:, :, q:].reshape(n_train, fj)
    denom = eigen_corr + damping
    act_wide = rot_au.astype(f32)
    group = 4

    def score_group(first):
        seq_ids = first + jnp.arange(group, dtype=jnp.int32)
        member = (query_seq[:, None] == seq_ids[None, :]).astype(bf16)
        weighted = (member[:, :, None] * rot_gq[:, None, :]).reshape(n_query, group * fi)
        outer = lax.dot_general(
            weighted, rot_aq, (((0,), (0,)), ((), ())), preferred_element_type=f32
        )
        precond = (outer.reshape(group, fi, fj) / denom[None, :, :]).astype(bf16)
        mapped = jnp.einsum("ui,sij->usj", rot_gu, precond, preferred_element_type=f32)
        return jnp.sum(mapped * act_wide[:, None, :], axis=2).T

    starts = jnp.arange(S // group, dtype=jnp.int32) * group
    partial_scores = lax.map(score_group, starts).reshape(S, n_train) / D
    doc_table = (train_doc[:, None] == jnp.arange(DOCS, dtype=jnp.int32)[None, :]).astype(f32)
    counts = jnp.sum(doc_table, axis=0)
    doc_part = jnp.dot(partial_scores, doc_table, precision=lax.Precision.HIGHEST)

    lanes = nzl * t
    p = partial_scores.reshape(S, nzl, nx, t)
    p = jnp.moveaxis(p, 2, 0).reshape(nx, S, lanes)
    d = jnp.broadcast_to(doc_part.reshape(1, -1, lanes), (nx, S * DOCS // lanes, lanes))
    p = jnp.concatenate([p, d, jnp.zeros_like(d)], axis=1)
    p = jnp.broadcast_to(p[None], (nyc,) + p.shape).reshape((nyc * nx,) + p.shape[1:])
    p = jnp.sum(exchange(p, ("y", "c", "x")), axis=0)
    d = p[S : S + S * DOCS // lanes].reshape(S, DOCS)
    p = jnp.swapaxes(p[:S].reshape(S, nzl, t), 0, 1)
    p = jnp.concatenate([p, jnp.broadcast_to(d[None], (nzl, S, DOCS))], axis=2)
    p = jnp.broadcast_to(p[None], (nzh,) + p.shape).reshape(nzh * nzl, -1, 128)
    p = jnp.sum(exchange(p, ("zh", "zl")), axis=0).reshape(S, t + DOCS)
    return (p[:, :t], p[:, t:] / counts[None, :])


def solution(mesh):
    fine = Mesh(mesh.devices.reshape(2, 4, 2, 8, 4), ROW + COL)
    in_specs = (
        P(ROW, COL),
        P(COL, ROW),
        P(ROW, COL),
        P(COL, ROW),
        P(COL, ROW),
        P(ROW, COL),
        P(ROW, COL),
        P(),
        P(),
        P(),
    )
    out_specs = (P(None, COL), P())
    return jax.shard_map(body, mesh=fine, in_specs=in_specs, out_specs=out_specs, check_vma=False)
```

```python
import jax
import jax.numpy as jnp
from jax import lax
from jax.experimental import pallas as pl
from jax.experimental.pallas import tpu as pltpu
from jax.sharding import Mesh, PartitionSpec as P


D = 8192
S = 32
DOCS = 16
ROW = ("zh", "y", "c")
COL = ("zl", "x")
GROUP = 4


def spread(v, axes):
    n = lax.axis_size(axes)
    return lax.all_to_all(jnp.broadcast_to(v[None], (n,) + v.shape), axes, 0, 0, tiled=True)


def exchange(parts, axes):
    return lax.all_to_all(parts, axes, 0, 0, tiled=True)


def split(v):
    hi = lax.reduce_precision(v, 8, 7)
    return hi.astype(jnp.bfloat16), (v - hi).astype(jnp.bfloat16)


def shift(v, axis, k):
    n = lax.axis_size(axis)
    return lax.ppermute(v, axis, [(i, (i + k) % n) for i in range(n)])


def around(v, axis):
    n = lax.axis_size(axis)
    return jnp.stack([v] + [shift(v, axis, n - k) for k in range(1, n)])


def turn(v, axis):
    n = lax.axis_size(axis)
    return lax.dynamic_slice_in_dim(
        jnp.concatenate([v, v[: n - 1]], axis=0), (n - lax.axis_index(axis)) % n, n, 0
    )


def score_kernel(seq_ref, table_ref, gq_ref, gu_ref, aqt_ref, aut_ref, rden_ref, out_ref, p_ref, sum_ref):
    f32, bf16 = jnp.float32, jnp.bfloat16
    fj, _ = rden_ref.shape
    seq = seq_ref[...]
    gq = gq_ref[...]
    aqt = aqt_ref[...]

    def precondition(first, slot):
        for k in range(GROUP):
            weighted = jnp.where(seq == first + k, aqt, jnp.zeros_like(aqt))
            outer = jnp.dot(weighted, gq, preferred_element_type=f32)
            p_ref[slot, k * fj : (k + 1) * fj, :] = (outer * rden_ref[...]).astype(bf16)

    def reduce(first, slot):
        mapped = lax.dot_general(
            p_ref[slot], gu_ref[...], (((1,), (1,)), ((), ())), preferred_element_type=f32
        )
        for k in range(GROUP):
            row = jnp.sum(mapped[k * fj : (k + 1) * fj] * aut_ref[...], axis=0, keepdims=True) / D
            sum_ref[pl.ds(first + k, 1), :] = row

    precondition(0, 0)

    def step(i, carry):
        first = i * (2 * GROUP)
        precondition(first + GROUP, 1)
        reduce(first, 0)
        precondition(first + 2 * GROUP, 0)
        reduce(first + GROUP, 1)
        return carry

    lax.fori_loop(0, S // (2 * GROUP) - 1, step, 0)
    precondition(S - GROUP, 1)
    reduce(S - 2 * GROUP, 0)
    reduce(S - GROUP, 1)
    docs = jnp.zeros((8, 128), f32)
    for g in range(S // 8):
        for x in range(out_ref.shape[0]):
            docs += jnp.dot(
                sum_ref[8 * g : 8 * g + 8, 128 * x : 128 * (x + 1)],
                table_ref[g, x],
                precision=lax.Precision.HIGHEST,
                preferred_element_type=f32,
            )
    for x in range(out_ref.shape[0]):
        out_ref[x, :S, :] = sum_ref[:, 128 * x : 128 * (x + 1)].astype(bf16)
        out_ref[x, S:, :] = docs.astype(bf16)


def partial_scores(seq, table, gq, gu, aqt, aut, rden):
    fj, fi = rden.shape
    vmem = pl.BlockSpec(memory_space=pltpu.VMEM)
    return pl.pallas_call(
        score_kernel,
        out_shape=jax.ShapeDtypeStruct((table.shape[1], S + 8, 128), jnp.bfloat16),
        in_specs=[vmem] * 7,
        out_specs=vmem,
        scratch_shapes=[
            pltpu.VMEM((2, GROUP * fj, fi), jnp.bfloat16),
            pltpu.VMEM((S, gu.shape[0]), jnp.float32),
        ],
        compiler_params=pltpu.CompilerParams(vmem_limit_bytes=40 * 1024 * 1024),
        name="partial_scores",
    )(seq, table, gq, gu, aqt, aut, rden)


def pack_kernel(total_ref, out_ref):
    total = jnp.concatenate([total_ref[...], jnp.zeros((128 - S - 8, 128), jnp.float32)], axis=0)
    turned = jnp.transpose(total)
    lane = lax.broadcasted_iota(jnp.int32, (DOCS, 128), 1)
    docs = jnp.zeros((DOCS, 128), jnp.float32)
    for g in range(S // 8):
        first = S + 8 * g
        moved = turned[DOCS * g : DOCS * (g + 1)]
        moved = pltpu.roll(moved, 8 * g, 1) if g else moved
        docs = jnp.where((lane >= first) & (lane < first + 8), moved, docs)
    for z in range(8):
        block = jnp.where(lane < S, turned[16 * z : 16 * z + 16], docs)
        block = jnp.where(lane[:8] < 2 * S, block[:8], pltpu.roll(block[8:], 2 * S, 1))
        for h in range(out_ref.shape[0] // 8):
            out_ref[8 * h + z] = block


def pack(total, nz):
    vmem = pl.BlockSpec(memory_space=pltpu.VMEM)
    return pl.pallas_call(
        pack_kernel,
        out_shape=jax.ShapeDtypeStruct((nz, 8, 128), jnp.float32),
        in_specs=[vmem],
        out_specs=vmem,
        name="pack",
    )(total)


def body(
    query_grads,
    query_acts,
    train_grads,
    train_acts,
    grad_basis,
    act_basis,
    eigen_corr,
    damping,
    query_seq,
    train_doc,
):
    bf16, f32 = jnp.bfloat16, jnp.float32
    n_query, n_train = query_seq.shape[0], train_doc.shape[0]
    nx, nzl, nzh = lax.axis_size("x"), lax.axis_size("zl"), lax.axis_size("zh")
    nyc = lax.axis_size(("y", "c"))
    q, t = query_acts.shape[0], train_acts.shape[0]
    n = q + t
    fi, fj = eigen_corr.shape

    a = spread(jnp.concatenate([query_acts, train_acts], axis=0), "zl")
    a = spread(a, "x")
    act_part = jnp.dot(a.reshape(-1, a.shape[-1]), act_basis, preferred_element_type=f32)
    act_part = act_part.astype(bf16).reshape(nyc, -1, fj)
    a = exchange(act_part, ("y", "c"))
    a = jnp.sum(a.astype(f32), axis=0)
    a = (a + lax.ppermute(a, "zh", [(0, 1), (1, 0)])).astype(bf16)
    a = around(a, "y")
    a = lax.all_gather(a, "c")
    acts = turn(jnp.swapaxes(a, 0, 1), "y").reshape(nx, nzl, n, fj)

    g = jnp.concatenate(
        [query_grads[:q], train_grads[:t], query_grads[q:], train_grads[t:]], axis=0
    )
    other = lax.ppermute(g, "zh", [(0, 1), (1, 0)])
    first = lax.axis_index("zh") == 0
    g = jnp.concatenate([jnp.where(first, g, other), jnp.where(first, other, g)], axis=0)
    g = around(g, "y")
    g = lax.all_gather(g, "c")
    g = g.reshape(n_query + n_train, -1)
    grad_part = jnp.dot(g, grad_basis, preferred_element_type=f32)
    grad_part = grad_part.astype(bf16).reshape(nx, -1, fi)
    x = lax.axis_index("x")
    own = [lax.dynamic_index_in_dim(grad_part, (x + k) % nx, 0, False) for k in range(nx)]
    got = [own[0]] + [shift(own[k], "x", k) for k in (1, nx - 1, 2)]
    g = sum(v.astype(f32) for v in got)
    g_hi, g_lo = split(g.reshape(nzl, n, fi))
    g = exchange(jnp.concatenate([g_hi, g_lo[:, :q]], axis=1), "zl").astype(f32)
    g = jnp.sum(g, axis=0)
    g = jnp.concatenate([g[:q] + g[n:], g[q:n]], axis=0).astype(bf16)
    g = spread(g, "zl").reshape(-1, fi)
    g = spread(g, "x")
    g = g.reshape(2, -1, nzh, 2, n, fi)
    grads = turn(jnp.moveaxis(g, 1, 0), "y")
    grads = jnp.transpose(grads, (1, 3, 2, 0, 4, 5))

    rot_gq = grads[..., :q, :].reshape(n_query, fi)
    rot_gu = grads[..., q:, :].reshape(n_train, fi)
    rden = (1.0 / (eigen_corr + damping)).T
    aqt = acts[:, :, :q].reshape(n_query, fj).T
    aut = acts[:, :, q:].reshape(n_train, fj).astype(f32).T
    seq = jnp.swapaxes(query_seq.reshape(nzl, nx, q), 0, 1).reshape(1, n_query)
    doc = jnp.swapaxes(train_doc.reshape(nzl, nx, t), 0, 1).reshape(nx, nzl * t)
    ids = jnp.arange(DOCS, dtype=jnp.int32)
    lanes = jnp.arange(128, dtype=jnp.int32)
    place = jnp.arange(S // 8, dtype=jnp.int32)[:, None, None, None] * DOCS
    table = (doc[None, :, :, None] + place == lanes).astype(f32)
    counts = jnp.sum((train_doc[:, None] == ids[None, :]).astype(f32), axis=0)
    p = partial_scores(seq, table, rot_gq, rot_gu, aqt, aut, rden)

    p = jnp.broadcast_to(p[None], (nyc,) + p.shape).reshape((nyc * nx,) + p.shape[1:])
    p = exchange(p, ("y", "c", "x"))
    p = pack(jnp.sum(p.astype(f32), axis=0), nzh * nzl)
    p = exchange(p, ("zh", "zl"))
    p = jnp.sum(p, axis=0)
    p = jnp.concatenate([p[:, : 2 * S], p[:, 2 * S :]], axis=0)
    return (p[:, :S].T, (p[:, S:] / counts[:, None]).T)


def solution(mesh):
    fine = Mesh(mesh.devices.reshape(2, 4, 2, 8, 4), ROW + COL)
    in_specs = (
        P(ROW, COL),
        P(COL, ROW),
        P(ROW, COL),
        P(COL, ROW),
        P(COL, ROW),
        P(ROW, COL),
        P(ROW, COL),
        P(),
        P(),
        P(),
    )
    out_specs = (P(None, COL), P())
    return jax.shard_map(body, mesh=fine, in_specs=in_specs, out_specs=out_specs, check_vma=False)
```

```python
import jax
import jax.numpy as jnp
from jax import lax
from jax.experimental import pallas as pl
from jax.experimental.pallas import tpu as pltpu
from jax.sharding import Mesh, PartitionSpec as P


D = 8192
S = 32
DOCS = 16
ROW = ("zh", "y", "c")
COL = ("zl", "x")
GROUP = 8


def spread(v, axes):
    n = lax.axis_size(axes)
    return lax.all_to_all(jnp.broadcast_to(v[None], (n,) + v.shape), axes, 0, 0, tiled=True)


def exchange(parts, axes):
    return lax.all_to_all(parts, axes, 0, 0, tiled=True)


def split(v):
    hi = lax.reduce_precision(v, 8, 7)
    return hi.astype(jnp.bfloat16), (v - hi).astype(jnp.bfloat16)


def shift(v, axis, k):
    n = lax.axis_size(axis)
    return lax.ppermute(v, axis, [(i, (i + k) % n) for i in range(n)])


def meet(v, axis, partner, first):
    other = lax.ppermute(v, axis, list(enumerate(partner)))
    return jnp.concatenate([jnp.where(first, v, other), jnp.where(first, other, v)], axis=0)


def score_kernel(seq_ref, table_ref, gq_ref, gu_ref, aqt_ref, aut_ref, rden_ref, out_ref, p_ref, sum_ref):
    f32, bf16 = jnp.float32, jnp.bfloat16
    fj, _ = rden_ref.shape
    seq = seq_ref[...]
    gq = gq_ref[...]
    aqt = aqt_ref[...]

    def precondition(first, slot):
        for k in range(GROUP):
            weighted = jnp.where(seq == jnp.asarray(first + k).astype(f32), aqt, jnp.zeros_like(aqt))
            outer = jnp.dot(weighted, gq, preferred_element_type=f32)
            p_ref[slot, k * fj : (k + 1) * fj, :] = (outer * rden_ref[...]).astype(bf16)

    def reduce(first, slot):
        mapped = lax.dot_general(
            p_ref[slot], gu_ref[...], (((1,), (1,)), ((), ())), preferred_element_type=f32
        )
        for k in range(GROUP):
            row = jnp.sum(mapped[k * fj : (k + 1) * fj] * aut_ref[...], axis=0, keepdims=True) / D
            sum_ref[pl.ds(first + k, 1), :] = row

    precondition(0, 0)

    def step(i, carry):
        first = i * (2 * GROUP)
        precondition(first + GROUP, 1)
        reduce(first, 0)
        precondition(first + 2 * GROUP, 0)
        reduce(first + GROUP, 1)
        return carry

    lax.fori_loop(0, S // (2 * GROUP) - 1, step, 0)
    precondition(S - GROUP, 1)
    reduce(S - 2 * GROUP, 0)
    reduce(S - GROUP, 1)
    docs = jnp.zeros((8, 128), f32)
    for g in range(S // 8):
        for m in range(sum_ref.shape[1] // 128):
            docs += jnp.dot(
                sum_ref[8 * g : 8 * g + 8, 128 * m : 128 * (m + 1)],
                table_ref[g, m],
                precision=lax.Precision.HIGHEST,
                preferred_element_type=f32,
            )
    half = S // 2
    low = lax.broadcasted_iota(jnp.int32, (half, 128), 1) < 64
    for m in range(sum_ref.shape[1] // 128):
        a = sum_ref[:half, 128 * m : 128 * (m + 1)]
        b = sum_ref[half:, 128 * m : 128 * (m + 1)]
        even = jnp.where(low, a, pltpu.roll(b, 64, 1)).astype(bf16)
        odd = jnp.where(low, pltpu.roll(a, 64, 1), b).astype(bf16)
        for z, rows in ((2 * m, even), (2 * m + 1, odd)):
            for h in range(out_ref.shape[0] // 8):
                out_ref[8 * h + z, :half, :] = rows
                out_ref[8 * h + z, half:, :] = docs.astype(bf16)


def partial_scores(seq, table, gq, gu, aqt, aut, rden, nz):
    fj, fi = rden.shape
    vmem = pl.BlockSpec(memory_space=pltpu.VMEM)
    return pl.pallas_call(
        score_kernel,
        out_shape=jax.ShapeDtypeStruct((nz, S // 2 + 8, 128), jnp.bfloat16),
        in_specs=[vmem] * 7,
        out_specs=vmem,
        scratch_shapes=[
            pltpu.VMEM((2, GROUP * fj, fi), jnp.bfloat16),
            pltpu.VMEM((S, gu.shape[0]), jnp.float32),
        ],
        compiler_params=pltpu.CompilerParams(vmem_limit_bytes=40 * 1024 * 1024),
        name="partial_scores",
    )(seq, table, gq, gu, aqt, aut, rden)


def pack_kernel(total_ref, out_ref):
    half = S // 2
    rows = total_ref.shape[0]
    total = jnp.concatenate([total_ref[...], jnp.zeros((128 - rows, 128), jnp.float32)], axis=0)
    turned = jnp.transpose(total)
    lane = lax.broadcasted_iota(jnp.int32, (DOCS, 128), 1)
    docs = jnp.zeros((DOCS, 128), jnp.float32)
    for g in range(S // 8):
        first = S + 8 * g
        moved = pltpu.roll(turned[DOCS * g : DOCS * (g + 1)], half + 8 * g, 1)
        docs = jnp.where((lane >= first) & (lane < first + 8), moved, docs)
    for x in range(4):
        block = jnp.where(lane < S, pltpu.roll(turned[64 + 16 * x : 80 + 16 * x], half, 1), docs)
        block = jnp.where(lane < half, turned[16 * x : 16 * x + 16], block)
        block = jnp.where(lane[:8] < 2 * S, block[:8], pltpu.roll(block[8:], 2 * S, 1))
        for h in range(out_ref.shape[0] // 4):
            out_ref[4 * h + x] = block


def pack(total, n):
    vmem = pl.BlockSpec(memory_space=pltpu.VMEM)
    return pl.pallas_call(
        pack_kernel,
        out_shape=jax.ShapeDtypeStruct((n, 8, 128), jnp.float32),
        in_specs=[vmem],
        out_specs=vmem,
        name="pack",
    )(total)


def body(
    query_grads,
    query_acts,
    train_grads,
    train_acts,
    grad_basis,
    act_basis,
    eigen_corr,
    damping,
    query_seq,
    train_doc,
):
    bf16, f32 = jnp.bfloat16, jnp.float32
    n_query, n_train = query_seq.shape[0], train_doc.shape[0]
    nx, nzl, nzh = lax.axis_size("x"), lax.axis_size("zl"), lax.axis_size("zh")
    nyc = lax.axis_size(("y", "c"))
    q, t = query_acts.shape[0], train_acts.shape[0]
    n = q + t
    fi, fj = eigen_corr.shape

    a = spread(jnp.concatenate([query_acts, train_acts], axis=0), "zl")
    a = spread(a, "x")
    act_part = jnp.dot(a.reshape(-1, a.shape[-1]), act_basis, preferred_element_type=f32)
    act_part = act_part.reshape(nyc, -1, fj)
    a = exchange(act_part, ("y", "c"))
    a = jnp.sum(a.astype(f32), axis=0)
    a = (a + lax.ppermute(a, "zh", [(0, 1), (1, 0)])).astype(bf16)
    y = lax.axis_index("y")
    a = meet(a[None], "y", (1, 0, 3, 2), y % 2 == 0)
    a = meet(a, "y", (3, 2, 1, 0), y < 2)
    a = lax.all_gather(a, "c")
    acts = jnp.swapaxes(a, 0, 1).reshape(nx, nzl, n, fj)

    g = jnp.concatenate(
        [query_grads[:q], train_grads[:t], query_grads[q:], train_grads[t:]], axis=0
    )
    other = lax.ppermute(g, "zh", [(0, 1), (1, 0)])
    first = lax.axis_index("zh") == 0
    g = jnp.concatenate([jnp.where(first, g, other), jnp.where(first, other, g)], axis=0)
    g = g.reshape(nzh, -1, fj)
    g = meet(g, "y", (1, 0, 3, 2), y % 2 == 0)
    g = meet(g, "y", (3, 2, 1, 0), y < 2)
    g = lax.all_gather(g, "c")
    g = g.reshape(n_query + n_train, -1)
    grad_part = jnp.dot(g, grad_basis, preferred_element_type=f32)
    grad_part = grad_part.astype(bf16).reshape(nx, -1, fi)
    x = lax.axis_index("x")
    own = [lax.dynamic_index_in_dim(grad_part, (x + k) % nx, 0, False) for k in range(nx)]
    got = [own[0]] + [shift(own[k], "x", k) for k in (1, nx - 1, 2)]
    g = sum(v.astype(f32) for v in got)
    g_hi, g_lo = split(g.reshape(nzl, n, fi))
    g = exchange(jnp.concatenate([g_hi, g_lo[:, :q]], axis=1), "zl").astype(f32)
    g = jnp.sum(g, axis=0)
    g = jnp.concatenate([g[:q] + g[n:], g[q:n]], axis=0).astype(bf16)
    g = spread(g, "zl").reshape(-1, fi)
    g = spread(g, "x")
    g = g.reshape(2, -1, nzh, 2, n, fi)
    grads = jnp.transpose(g, (2, 1, 0, 3, 4, 5))

    rot_gq = grads[..., :q, :].reshape(n_query, fi)
    rot_gu = grads[..., q:, :].reshape(n_train, fi)
    rden = (1.0 / (eigen_corr + damping)).T
    acts = jnp.swapaxes(acts, 0, 1)
    aqt = acts[:, :, :q].reshape(n_query, fj).T
    aut = acts[:, :, q:].reshape(n_train, fj).astype(f32).T
    seq = query_seq.astype(f32).reshape(1, n_query)
    doc = train_doc.reshape(-1, 128)
    ids = jnp.arange(DOCS, dtype=jnp.int32)
    lanes = jnp.arange(128, dtype=jnp.int32)
    place = jnp.arange(S // 8, dtype=jnp.int32)[:, None, None, None] * DOCS
    table = (doc[None, :, :, None] + place == lanes).astype(f32)
    counts = jnp.sum((train_doc[:, None] == ids[None, :]).astype(f32), axis=0)
    p = partial_scores(seq, table, rot_gq, rot_gu, aqt, aut, rden, nzh * nzl)

    p = exchange(p, ("zh", "zl"))
    p = pack(jnp.sum(p.astype(f32), axis=0), nyc * nx)
    p = exchange(p, ("y", "c", "x"))
    p = jnp.sum(p, axis=0)
    p = jnp.concatenate([p[:, : 2 * S], p[:, 2 * S :]], axis=0)
    return (p[:, :S].T, (p[:, S:] / counts[:, None]).T)


def solution(mesh):
    fine = Mesh(mesh.devices.reshape(2, 4, 2, 8, 4), ROW + COL)
    in_specs = (
        P(ROW, COL),
        P(COL, ROW),
        P(ROW, COL),
        P(COL, ROW),
        P(COL, ROW),
        P(ROW, COL),
        P(ROW, COL),
        P(),
        P(),
        P(),
    )
    out_specs = (P(None, COL), P())
    return jax.shard_map(body, mesh=fine, in_specs=in_specs, out_specs=out_specs, check_vma=False)
```

```python
import jax
import jax.numpy as jnp
from jax import lax
from jax.experimental import pallas as pl
from jax.experimental.pallas import tpu as pltpu
from jax.sharding import Mesh, PartitionSpec as P


D = 8192
S = 32
DOCS = 16
ROW = ("zh", "y", "c")
COL = ("zl", "x")
GROUP = 8


def spread(v, axes):
    n = lax.axis_size(axes)
    return lax.all_to_all(jnp.broadcast_to(v[None], (n,) + v.shape), axes, 0, 0, tiled=True)


def exchange(parts, axes):
    return lax.all_to_all(parts, axes, 0, 0, tiled=True)


def split(v):
    hi = lax.reduce_precision(v, 8, 7)
    return hi.astype(jnp.bfloat16), (v - hi).astype(jnp.bfloat16)


def shift(v, axis, k):
    n = lax.axis_size(axis)
    return lax.ppermute(v, axis, [(i, (i + k) % n) for i in range(n)])


def meet(v, axis, partner, first):
    other = lax.ppermute(v, axis, list(enumerate(partner)))
    return jnp.concatenate([jnp.where(first, v, other), jnp.where(first, other, v)], axis=0)


def score_kernel(seq_ref, table_ref, gq_ref, gu_ref, aqt_ref, aut_ref, rden_ref, out_ref, p_ref, sum_ref):
    f32, bf16 = jnp.float32, jnp.bfloat16
    fj, _ = rden_ref.shape
    seq = seq_ref[...]
    gq = gq_ref[...]
    aqt = aqt_ref[...]

    def precondition(first, slot):
        for k in range(GROUP):
            weighted = jnp.where(seq == jnp.asarray(first + k).astype(f32), aqt, jnp.zeros_like(aqt))
            outer = jnp.dot(weighted, gq, preferred_element_type=f32)
            p_ref[slot, k * fj : (k + 1) * fj, :] = (outer * rden_ref[...]).astype(bf16)

    def reduce(first, slot):
        mapped = lax.dot_general(
            p_ref[slot], gu_ref[...], (((1,), (1,)), ((), ())), preferred_element_type=f32
        )
        for k in range(GROUP):
            row = jnp.sum(mapped[k * fj : (k + 1) * fj] * aut_ref[...], axis=0, keepdims=True) / D
            sum_ref[pl.ds(first + k, 1), :] = row

    precondition(0, 0)

    def step(i, carry):
        first = i * (2 * GROUP)
        precondition(first + GROUP, 1)
        reduce(first, 0)
        precondition(first + 2 * GROUP, 0)
        reduce(first + GROUP, 1)
        return carry

    lax.fori_loop(0, S // (2 * GROUP) - 1, step, 0)
    precondition(S - GROUP, 1)
    reduce(S - 2 * GROUP, 0)
    reduce(S - GROUP, 1)
    docs = jnp.zeros((8, 128), f32)
    for g in range(S // 8):
        for m in range(sum_ref.shape[1] // 128):
            docs += jnp.dot(
                sum_ref[8 * g : 8 * g + 8, 128 * m : 128 * (m + 1)],
                table_ref[g, m],
                precision=lax.Precision.HIGHEST,
                preferred_element_type=f32,
            )
    rest = pltpu.roll(docs - docs.astype(bf16).astype(f32), 64, 1)
    docs = jnp.where(lax.broadcasted_iota(jnp.int32, docs.shape, 1) < 64, docs, rest)
    half = S // 2
    low = lax.broadcasted_iota(jnp.int32, (half, 128), 1) < 64
    for m in range(sum_ref.shape[1] // 128):
        a = sum_ref[:half, 128 * m : 128 * (m + 1)]
        b = sum_ref[half:, 128 * m : 128 * (m + 1)]
        even = jnp.where(low, a, pltpu.roll(b, 64, 1)).astype(bf16)
        odd = jnp.where(low, pltpu.roll(a, 64, 1), b).astype(bf16)
        for z, rows in ((2 * m, even), (2 * m + 1, odd)):
            for h in range(out_ref.shape[0] // 8):
                out_ref[8 * h + z, :half, :] = rows
                out_ref[8 * h + z, half:, :] = docs.astype(bf16)


def partial_scores(seq, table, gq, gu, aqt, aut, rden, nz):
    fj, fi = rden.shape
    vmem = pl.BlockSpec(memory_space=pltpu.VMEM)
    return pl.pallas_call(
        score_kernel,
        out_shape=jax.ShapeDtypeStruct((nz, S // 2 + 8, 128), jnp.bfloat16),
        in_specs=[vmem] * 7,
        out_specs=vmem,
        scratch_shapes=[
            pltpu.VMEM((2, GROUP * fj, fi), jnp.bfloat16),
            pltpu.VMEM((S, gu.shape[0]), jnp.float32),
        ],
        compiler_params=pltpu.CompilerParams(vmem_limit_bytes=40 * 1024 * 1024),
        name="partial_scores",
    )(seq, table, gq, gu, aqt, aut, rden)


def pack_kernel(total_ref, out_ref):
    half = S // 2
    rows = total_ref.shape[0]
    docs = total_ref[half:, :] + pltpu.roll(total_ref[half:, :], 64, 1)
    empty = jnp.zeros((128 - rows, 128), jnp.float32)
    total = jnp.concatenate([total_ref[:half, :], docs, empty], axis=0)
    turned = jnp.transpose(total)
    lane = lax.broadcasted_iota(jnp.int32, (DOCS, 128), 1)
    docs = jnp.zeros((DOCS, 128), jnp.float32)
    for g in range(S // 8):
        first = S + 8 * g
        moved = pltpu.roll(turned[DOCS * g : DOCS * (g + 1)], half + 8 * g, 1)
        docs = jnp.where((lane >= first) & (lane < first + 8), moved, docs)
    for x in range(4):
        block = jnp.where(lane < S, pltpu.roll(turned[64 + 16 * x : 80 + 16 * x], half, 1), docs)
        block = jnp.where(lane < half, turned[16 * x : 16 * x + 16], block)
        block = jnp.where(lane[:8] < 2 * S, block[:8], pltpu.roll(block[8:], 2 * S, 1))
        for h in range(out_ref.shape[0] // 4):
            out_ref[4 * h + x] = block


def pack(total, n):
    vmem = pl.BlockSpec(memory_space=pltpu.VMEM)
    return pl.pallas_call(
        pack_kernel,
        out_shape=jax.ShapeDtypeStruct((n, 8, 128), jnp.float32),
        in_specs=[vmem],
        out_specs=vmem,
        name="pack",
    )(total)


def body(
    query_grads,
    query_acts,
    train_grads,
    train_acts,
    grad_basis,
    act_basis,
    eigen_corr,
    damping,
    query_seq,
    train_doc,
):
    bf16, f32 = jnp.bfloat16, jnp.float32
    n_query, n_train = query_seq.shape[0], train_doc.shape[0]
    nx, nzl, nzh = lax.axis_size("x"), lax.axis_size("zl"), lax.axis_size("zh")
    nyc = lax.axis_size(("y", "c"))
    q, t = query_acts.shape[0], train_acts.shape[0]
    n = q + t
    fi, fj = eigen_corr.shape

    a = spread(jnp.concatenate([query_acts, train_acts], axis=0), "zl")
    a = spread(a, "x")
    act_part = jnp.dot(a.reshape(-1, a.shape[-1]), act_basis, preferred_element_type=f32)
    act_part = act_part.reshape(nyc, -1, fj)
    a = exchange(act_part, ("y", "c"))
    a = jnp.sum(a.astype(f32), axis=0)
    a = (a + lax.ppermute(a, "zh", [(0, 1), (1, 0)])).astype(bf16)
    y = lax.axis_index("y")
    a = meet(a[None], "y", (1, 0, 3, 2), y % 2 == 0)
    a = meet(a, "y", (3, 2, 1, 0), y < 2)
    a = lax.all_gather(a, "c")
    acts = jnp.swapaxes(a, 0, 1).reshape(nx, nzl, n, fj)

    g = jnp.concatenate(
        [query_grads[:q], train_grads[:t], query_grads[q:], train_grads[t:]], axis=0
    )
    other = lax.ppermute(g, "zh", [(0, 1), (1, 0)])
    first = lax.axis_index("zh") == 0
    g = jnp.concatenate([jnp.where(first, g, other), jnp.where(first, other, g)], axis=0)
    g = g.reshape(nzh, -1, fj)
    g = meet(g, "y", (1, 0, 3, 2), y % 2 == 0)
    g = meet(g, "y", (3, 2, 1, 0), y < 2)
    g = lax.all_gather(g, "c")
    g = g.reshape(n_query + n_train, -1)
    grad_part = jnp.dot(g, grad_basis, preferred_element_type=f32)
    grad_part = grad_part.astype(bf16).reshape(nx, -1, fi)
    x = lax.axis_index("x")
    own = [lax.dynamic_index_in_dim(grad_part, (x + k) % nx, 0, False) for k in range(nx)]
    got = [own[0]] + [shift(own[k], "x", k) for k in (1, nx - 1, 2)]
    g = sum(v.astype(f32) for v in got)
    g_hi, g_lo = split(g.reshape(nzl, n, fi))
    g = exchange(jnp.concatenate([g_hi, g_lo[:, :q]], axis=1), "zl").astype(f32)
    g = jnp.sum(g, axis=0)
    g = jnp.concatenate([g[:q] + g[n:], g[q:n]], axis=0).astype(bf16)
    g = spread(g, "zl").reshape(-1, fi)
    g = spread(g, "x")
    g = g.reshape(2, -1, nzh, 2, n, fi)
    grads = jnp.transpose(g, (2, 1, 0, 3, 4, 5))

    rot_gq = grads[..., :q, :].reshape(n_query, fi)
    rot_gu = grads[..., q:, :].reshape(n_train, fi)
    rden = (1.0 / (eigen_corr + damping)).T
    acts = jnp.swapaxes(acts, 0, 1)
    aqt = acts[:, :, :q].reshape(n_query, fj).T
    aut = acts[:, :, q:].reshape(n_train, fj).astype(f32).T
    seq = query_seq.astype(f32).reshape(1, n_query)
    doc = train_doc.reshape(-1, 128)
    ids = jnp.arange(DOCS, dtype=jnp.int32)
    lanes = jnp.arange(128, dtype=jnp.int32)
    place = jnp.arange(S // 8, dtype=jnp.int32)[:, None, None, None] * DOCS
    table = (doc[None, :, :, None] + place == lanes).astype(f32)
    counts = jnp.sum((train_doc[:, None] == ids[None, :]).astype(f32), axis=0)
    p = partial_scores(seq, table, rot_gq, rot_gu, aqt, aut, rden, nzh * nzl)

    p = exchange(p, ("zh", "zl"))
    p = pack(jnp.sum(p.astype(f32), axis=0), nyc * nx)
    p = exchange(p, ("y", "c", "x"))
    p = jnp.sum(p, axis=0)
    p = jnp.concatenate([p[:, : 2 * S], p[:, 2 * S :]], axis=0)
    return (p[:, :S].T, (p[:, S:] / counts[:, None]).T)


def solution(mesh):
    fine = Mesh(mesh.devices.reshape(2, 4, 2, 8, 4), ROW + COL)
    in_specs = (
        P(ROW, COL),
        P(COL, ROW),
        P(ROW, COL),
        P(COL, ROW),
        P(COL, ROW),
        P(ROW, COL),
        P(ROW, COL),
        P(),
        P(),
        P(),
    )
    out_specs = (P(None, COL), P())
    return jax.shard_map(body, mesh=fine, in_specs=in_specs, out_specs=out_specs, check_vma=False)
```
